32 devices in a mesh: groups: 1, seq: 16 (over z, y, core), head: 2 (over x).
Axes of the slice: x: 2, y: 2, z: 4, core: 2. Of those that a mesh axis runs over, the one named last changes fastest.
Arguments:
- x_proj: bfloat16 [12288, 8192], P(('groups', 'seq'), 'head'), may hold values from -6 to 6
- z_gate: bfloat16 [12288, 8192], P(('groups', 'seq'), 'head'), may hold values from -6 to 6
- bc_proj: bfloat16 [12288, 8, 256], P(('groups', 'seq'), 'head'), may hold values from -6 to 6
- dt_proj: bfloat16 [12288, 128], P(('groups', 'seq'), 'head'), may hold values from -5 to 5
- dt_bias: float32 [128], P('head'), may hold values from -4 to -1
- decay_log: float32 [128], P('head'), may hold values from -10 to 1
- skip_gain: float32 [128], P('head'), may hold values from 0.5 to 2
- conv_x: float32 [4, 8192], P(None, 'head'), may hold values from -3 to 3
- bias_x: float32 [8192], P('head'), may hold values from -3 to 3
- conv_bc: float32 [4, 8, 256], P(None, 'head'), may hold values from -3 to 3
- bias_bc: float32 [8, 256], P('head'), may hold values from -3 to 3
- norm_gain: float32 [8192], P('head'), may hold values from 0.5 to 1.5
- seg_lengths: int32 [4], P('groups'), may hold values from 1 to 6144, 12288 in all
Outputs:
- mixed: bfloat16 [12288, 8192], P(('groups', 'seq'), 'head')
The draws below stay inside these ranges and needn't reach their ends.
Inputs may be any that keep to these rules, and one draw needn't show every extreme that they name: `seg_lengths`: the 4 rollouts fill the pack of 12288 tokens in order; the longest has exactly 6144 tokens.
All inputs are finite; a program needn't handle non-finite values.
Results may differ from the reference program's by a relative error of at most 0.0049.
Values may be sent and summed in bfloat16 or wider, within the bound.
A program may use at most 256 MiB of HBM per device.

```python
import math
import jax
import jax.numpy as jnp
import numpy as np
from jax import lax

HEADS = 128
HEAD_DIM = 64
STATE = 128
GROUPS = 8
CONV = 4
BLOCK = 128
DI = 8192
SEQ = 12288
NSEG = 4
MOST = 6144


def draw_dt_proj(key, part):
    values = jax.random.truncated_normal(key, -5.0, 5.0, (SEQ, HEADS), jnp.float32)
    return values.astype(jnp.bfloat16)


def level_of(key, dims, pieces, least, largest):
    def one(position, blocks):
        heights = jax.random.uniform(jax.random.fold_in(jax.random.fold_in(key, 6), position), (blocks,), jnp.float32, least / len(pieces), largest / len(pieces))
        return jnp.repeat(jnp.exp(heights), dims[position] // blocks).reshape((-1,) + (1,) * (len(dims) - position - 1))

    factor_of = one(*pieces[0])
    for cut in pieces[1:]:
        factor_of = factor_of * one(*cut)
    return factor_of


def profile(number_of, total, limit, lean):
    loads = [(1 << 20) // math.isqrt(rank ** lean) + 1 for rank in range(2, number_of + 1)]
    spare, given = total - limit - (number_of - 1), [1] * (number_of - 1)
    while spare > 0:
        free = [i for i in range(number_of - 1) if given[i] < limit]
        pool, budget = sum([loads[i] for i in free]), spare
        for i in free:
            extra = min(limit - given[i], max(1, budget * loads[i] // pool), spare)
            given[i] = given[i] + extra
            spare = spare - extra
    return np.array([limit] + given)


def ragged_sizes(rng, count, total, most, lean):
    if count == 2:
        one = jax.random.randint(rng, (), max(1, total - most), min(most, total - 1) + 1)
        return jnp.stack([one, total - one])
    tallies = jnp.asarray(profile(count, total, most, lean), jnp.int32)
    couples = (count - 1) // 2
    giver, taker = tallies[1:1 + 2 * couples:2], tallies[2:2 + 2 * couples:2]
    slack = jnp.minimum(giver - 1, most - taker)
    moved = jax.random.randint(jax.random.fold_in(rng, 1), (couples,), 0, 1 << 20) % (slack + 1)
    tallies = tallies.at[1:1 + 2 * couples:2].set(giver - moved).at[2:2 + 2 * couples:2].set(taker + moved)
    return tallies[jax.random.permutation(jax.random.fold_in(rng, 2), count)]


def normal_values(stream_key, extent, scale, limit, pieces=(), kind=jnp.bfloat16):
    level = level_of(stream_key, extent, pieces, -0.22, 0.18) if pieces else 1.0
    drawn = jax.random.normal(stream_key, extent, jnp.float32) * scale * level
    return jnp.minimum(jnp.maximum(drawn, -limit), limit).astype(kind)


def setup_inputs(seed: int = 0, part: int = 0) -> dict:
    splits = jax.random.split(jax.random.key(seed), 14)
    part_splits = jax.random.split(jax.random.fold_in(splits[13], part), 14)
    x_proj = normal_values(part_splits[0], (SEQ, DI), 1.0, 6.0, ((0, 16), (1, 2)))
    z_gate = normal_values(part_splits[1], (SEQ, DI), 1.0, 6.0, ((0, 16), (1, 2)))
    bc_proj = normal_values(part_splits[2], (SEQ, GROUPS, 2 * STATE), 1.0, 6.0, ((0, 16), (1, 2)))
    dt_proj = draw_dt_proj(jax.random.fold_in(jax.random.fold_in(splits[13], part), 71), part)
    dt_bias = jnp.clip(-4.0 + 3.0 * jax.random.uniform(splits[4], (HEADS,), jnp.float32) ** level_of(splits[4], (HEADS,), ((0, 2),), -0.2, 0.2), -4.0, -1.0)
    decay_log = jnp.clip(-10.0 + 11.0 * jax.random.uniform(splits[5], (HEADS,), jnp.float32) ** level_of(splits[5], (HEADS,), ((0, 2),), -0.2, 0.2), -10.0, 1.0)
    skip_gain = jnp.clip(0.5 + 1.5 * jax.random.uniform(splits[6], (HEADS,), jnp.float32) ** level_of(splits[6], (HEADS,), ((0, 2),), -0.2, 0.2), 0.5, 2.0)
    conv_x = normal_values(splits[7], (CONV, DI), 0.5, 3.0, ((1, 2),), jnp.float32)
    bias_x = normal_values(splits[8], (DI,), 0.5, 3.0, ((0, 2),), jnp.float32)
    conv_bc = normal_values(splits[9], (CONV, GROUPS, 2 * STATE), 0.5, 3.0, ((1, 2),), jnp.float32)
    bias_bc = normal_values(splits[10], (GROUPS, 2 * STATE), 0.5, 3.0, ((0, 2),), jnp.float32)
    norm_gain = jnp.clip(1.0 + 0.1 * jax.random.normal(splits[11], (DI,), jnp.float32), 0.5, 1.5)
    seg_lengths = ragged_sizes(part_splits[12], NSEG, SEQ, MOST, 2).astype(jnp.int32)
    return {"x_proj": x_proj, "z_gate": z_gate, "bc_proj": bc_proj, "dt_proj": dt_proj, "dt_bias": dt_bias, "decay_log": decay_log, "skip_gain": skip_gain, "conv_x": conv_x, "bias_x": bias_x, "conv_bc": conv_bc, "bias_bc": bias_bc, "norm_gain": norm_gain, "seg_lengths": seg_lengths}


def segment_of(seg_lengths, positions):
    starts = jnp.cumsum(seg_lengths) - seg_lengths
    hits = (starts[None, :] <= positions[:, None]).astype(jnp.int32)
    return (lax.optimization_barrier(jnp.sum(hits, axis=1)) - 1).astype(jnp.int32)

def conv_mix(extended, ext_segment, weight, bias):
    lookback = weight.shape[0] - 1
    length = extended.shape[0] - lookback
    own_seg = ext_segment[lookback:]
    trailing = (1,) * (extended.ndim - 1)
    total = bias.astype(jnp.float32)[None]
    for tap_index in range(weight.shape[0]):
        valid = (ext_segment[tap_index:tap_index + length] == own_seg).astype(jnp.float32).reshape((length,) + trailing)
        total = total + weight[tap_index].astype(jnp.float32)[None] * extended[tap_index:tap_index + length].astype(jnp.float32) * valid
    return jax.nn.silu(total)

def gated_norm(values, gate, gain, groups_here):
    gated = values * jax.nn.silu(gate.astype(jnp.float32))
    length = gated.shape[0]
    grouped = gated.reshape(length, groups_here, -1)
    meansq = lax.optimization_barrier(jnp.mean(grouped * grouped, axis=2, keepdims=True))
    normed = (grouped * lax.rsqrt(meansq + 1e-05)).reshape(length, -1)
    return (normed * gain[None]).astype(jnp.bfloat16)

def state_read(c_part, grouped):
    upper = grouped.astype(jnp.bfloat16)
    lower = (grouped - upper.astype(jnp.float32)).astype(jnp.bfloat16)
    c_float = c_part.astype(jnp.float32)
    first = jnp.einsum('tgn,grpn->tgrp', c_float, upper.astype(jnp.float32))
    second = jnp.einsum('tgn,grpn->tgrp', c_float, lower.astype(jnp.float32))
    return first + second

def block_step(state, inputs):
    values, b_part, c_part, step_size, log_decay, segment, previous = inputs
    length, heads_here, head_width = values.shape
    groups_here = b_part.shape[1]
    repeat = heads_here // groups_here
    cumulative = jnp.cumsum(log_decay, axis=0)
    causal = jnp.arange(length)[:, None] >= jnp.arange(length)[None, :]
    allowed = causal & (segment[:, None] == segment[None, :])
    columns = cumulative.T
    spread = jnp.where(allowed[None], columns[:, :, None] - columns[:, None, :], -jnp.inf)
    scores = jnp.einsum('tgn,sgn->gts', c_part.astype(jnp.float32), b_part.astype(jnp.float32))
    scores = jnp.repeat(scores, repeat, axis=0)
    weights = (scores * jnp.exp(spread) * step_size.T[:, None, :]).astype(jnp.bfloat16)
    output = jnp.einsum('hts,shp->thp', weights.astype(jnp.float32), values.astype(jnp.float32))
    alive = (segment == previous).astype(jnp.float32)
    grouped = state.reshape(groups_here, repeat, head_width, -1)
    carried = state_read(c_part, grouped).reshape(length, heads_here, head_width)
    output = output + (jnp.exp(cumulative) * alive[:, None])[:, :, None] * carried
    same_end = (segment == segment[-1]).astype(jnp.float32)
    tail_weight = jnp.exp(cumulative[-1][None, :] - cumulative) * same_end[:, None] * step_size
    scaled = (values.astype(jnp.float32) * tail_weight[:, :, None]).astype(jnp.bfloat16)
    update = jnp.einsum('sgrp,sgn->grpn', scaled.reshape(length, groups_here, repeat, head_width).astype(jnp.float32), b_part.astype(jnp.float32))
    state = (jnp.exp(cumulative[-1]) * alive[-1])[:, None, None] * state + update.reshape(state.shape)
    return (state, output)

def reference(x_proj, z_gate, bc_proj, dt_proj, dt_bias, decay_log, skip_gain, conv_x, bias_x, conv_bc, bias_bc, norm_gain, seg_lengths):
    lookback = conv_x.shape[0] - 1
    positions = jnp.arange(-lookback, SEQ, dtype=jnp.int32)
    segments = segment_of(seg_lengths, positions)
    zero_x = jnp.zeros((lookback,) + x_proj.shape[1:], x_proj.dtype)
    zero_bc = jnp.zeros((lookback,) + bc_proj.shape[1:], bc_proj.dtype)
    mixed_x = conv_mix(jnp.concatenate([zero_x, x_proj]), segments, conv_x, bias_x).astype(jnp.bfloat16)
    mixed_bc = conv_mix(jnp.concatenate([zero_bc, bc_proj]), segments, conv_bc, bias_bc).astype(jnp.bfloat16)
    step_size = jax.nn.softplus(dt_proj.astype(jnp.float32) + dt_bias[None])
    log_decay = -jnp.exp(decay_log)[None] * step_size
    own_segment = segments[lookback:]
    block_count = SEQ // BLOCK
    block_prev = segments[lookback - 1::BLOCK][:block_count]
    values = mixed_x.reshape(SEQ, HEADS, HEAD_DIM)
    inputs = (values.reshape(block_count, BLOCK, HEADS, HEAD_DIM), mixed_bc[:, :, :STATE].reshape(block_count, BLOCK, GROUPS, STATE), mixed_bc[:, :, STATE:].reshape(block_count, BLOCK, GROUPS, STATE), step_size.reshape(block_count, BLOCK, HEADS), log_decay.reshape(block_count, BLOCK, HEADS), own_segment.reshape(block_count, BLOCK), block_prev)
    final_state, output = lax.scan(block_step, jnp.zeros((HEADS, HEAD_DIM, STATE), jnp.float32), inputs)
    output = output.reshape(SEQ, HEADS, HEAD_DIM) + skip_gain[None, :, None] * values.astype(jnp.float32)
    return gated_norm(output.reshape(SEQ, DI), z_gate, norm_gain, GROUPS)
```

```python
import functools

import jax
import jax.numpy as jnp
from jax import lax
from jax.experimental import pallas as pl
from jax.experimental.pallas import tpu as pltpu
from jax.sharding import PartitionSpec as P

HEAD_DIM = 64
STATE = 128
BLOCK = 128
LANES = 128
TAIL = 16
LOG2E = 1.4426950408889634
MESH = pl.DeviceIdType.MESH
F32 = jnp.float32
BF16 = jnp.bfloat16


def segment_of(seg_lengths, positions):
    starts = jnp.cumsum(seg_lengths) - seg_lengths
    hits = (starts[None, :] <= positions[:, None]).astype(jnp.int32)
    return jnp.sum(hits, axis=1) - 1


def silu(u):
    half = 0.5 * u
    return half + half * jnp.tanh(half)


def mm(a, b, dims, precision=None):
    return lax.dot_general(a, b, (dims, ((), ())), precision=precision, preferred_element_type=F32)


def steps_of(dtp_ref, dtb_ref, dec_ref):
    raw = dtp_ref[...].astype(F32) + dtb_ref[...]
    dt = jnp.maximum(raw, 0.0) + jnp.log1p(jnp.exp(-jnp.abs(raw)))
    la = (-LOG2E * jnp.exp(dec_ref[...])) * dt
    s = lax.broadcasted_iota(jnp.int32, (BLOCK, BLOCK), 0)
    t = lax.broadcasted_iota(jnp.int32, (BLOCK, BLOCK), 1)
    upper = (s <= t).astype(F32)
    return dt, mm(la, upper, ((1,), (0,)), lax.Precision.HIGHEST)


def expand(value, e_ref):
    hi = value.astype(BF16)
    lo = (value - hi.astype(F32)).astype(BF16)
    return mm(jnp.concatenate([hi, lo], axis=0), e_ref[...], ((0,), (0,)))


def conv_into(dst, src, tail, halo, weight, bias, masks, first):
    width = dst.shape[1]

    @pl.when(first)
    def _():
        halo[0:8, :] = tail[TAIL - 8 : TAIL, :].astype(F32)

    @pl.when(jnp.logical_not(first))
    def _():
        halo[0:8, :] = halo[BLOCK : BLOCK + 8, :]

    for j in range(width // LANES):
        sl = slice(j * LANES, (j + 1) * LANES)
        own = src[:, sl].astype(F32)
        halo[8 : BLOCK + 8, sl] = own
        total = bias[0:1, sl] + weight[3:4, sl] * own
        for k in range(3):
            total = total + weight[k : k + 1, sl] * (halo[5 + k : 5 + k + BLOCK, sl] * masks[k])
        dst[:, sl] = silu(total).astype(BF16)


def local_kernel(
    x_ref, xt_ref, bc_ref, bct_ref, dtp_ref, cols_ref, rows_ref, dtb_ref, dec_ref,
    wx_ref, bx_ref, wbc_ref, bbc_ref, e_ref,
    xc_ref, bcc_ref, s_ref, d_ref, xhalo, bhalo, scaled, tailw,
):
    b = pl.program_id(1)
    first = b == 0
    masks = [jnp.broadcast_to(cols_ref[:, k : k + 1], (BLOCK, LANES)) for k in range(3)]
    conv_into(xc_ref, x_ref, xt_ref, xhalo, wx_ref, bx_ref, masks, first)
    conv_into(bcc_ref, bc_ref, bct_ref, bhalo, wbc_ref, bbc_ref, masks, first)
    dt, cum = steps_of(dtp_ref, dtb_ref, dec_ref)
    last = cum[:, BLOCK - 1 : BLOCK]
    tailw[...] = expand(jnp.exp2(last - cum) * dt * rows_ref[0, 1:2, :], e_ref)
    decay = expand(jnp.exp2(jnp.broadcast_to(last, cum.shape)) * rows_ref[0, 3:4, :], e_ref)[0:8]
    width = x_ref.shape[1]
    for j in range(width // LANES):
        sl = slice(j * LANES, (j + 1) * LANES)
        scaled[:, sl] = (xc_ref[:, sl].astype(F32) * tailw[:, sl]).astype(BF16)
    update = mm(bcc_ref[:, 0:STATE], scaled[...], ((0,), (0,)))

    @pl.when(first)
    def _():
        s_ref[...] = update
        d_ref[...] = decay

    @pl.when(jnp.logical_not(first))
    def _():
        s_ref[...] = decay[0:1] * s_ref[...] + update
        d_ref[...] = decay * d_ref[...]


def chain_kernel(chunks, s_ref, d_ref, in_ref, sendbuf, recvbuf, send_sem, recv_sem):
    peers = lax.axis_size("seq")
    me = lax.axis_index("seq")
    width = s_ref.shape[1] // chunks
    barrier = pltpu.get_barrier_semaphore()

    for peer in (lax.rem(me + peers - 1, peers), lax.rem(me + 1, peers)):
        pl.semaphore_signal(barrier, inc=1, device_id={"seq": peer}, device_id_type=MESH)
    pl.semaphore_wait(barrier, 2)

    def copy(k):
        return pltpu.make_async_remote_copy(
            src_ref=sendbuf.at[k],
            dst_ref=recvbuf.at[k],
            send_sem=send_sem.at[k],
            recv_sem=recv_sem.at[k],
            device_id={"seq": lax.rem(me + 1, peers)},
            device_id_type=MESH,
        )

    for k in range(chunks):
        sl = slice(k * width, (k + 1) * width)

        @pl.when(me == 0)
        def _():
            in_ref[:, sl] = jnp.zeros((STATE, width), BF16)
            sendbuf[k] = s_ref[:, sl].astype(BF16)

        @pl.when(me > 0)
        def _():
            copy(k).wait_recv()
            arrived = recvbuf[k]
            in_ref[:, sl] = arrived
            sendbuf[k] = (d_ref[0:1, sl] * arrived.astype(F32) + s_ref[:, sl]).astype(BF16)

        @pl.when(me < peers - 1)
        def _():
            copy(k).start()

    for k in range(chunks):

        @pl.when(me < peers - 1)
        def _():
            copy(k).wait_send()


def output_kernel(
    xc_ref, bcc_ref, z_ref, in_ref, dtp_ref, cols_ref, rows_ref, dtb_ref, dec_ref,
    skip_ref, gain_ref, e_ref, out_ref, state, cfac, tailw, scaled, carried, gated,
):
    b = pl.program_id(1)
    width = xc_ref.shape[1]

    @pl.when(b == 0)
    def _():
        state[...] = in_ref[...].astype(F32)

    dt, cum = steps_of(dtp_ref, dtb_ref, dec_ref)
    cfac[...] = expand(jnp.exp2(cum) * rows_ref[0, 2:3, :], e_ref)
    last = cum[:, BLOCK - 1 : BLOCK]
    tailw[...] = expand(jnp.exp2(last - cum) * dt * rows_ref[0, 1:2, :], e_ref)
    b_part = bcc_ref[:, 0:STATE]
    c_part = bcc_ref[:, STATE : 2 * STATE]
    carried[...] = mm(c_part, state[...].astype(BF16), ((1,), (0,)))
    scores = mm(c_part, b_part, ((1,), (1,)))
    t = lax.broadcasted_iota(jnp.int32, (BLOCK, BLOCK), 0)
    s = lax.broadcasted_iota(jnp.int32, (BLOCK, BLOCK), 1)
    allowed = (s <= t) & (cols_ref[:, 3:4] == rows_ref[0, 0:1, :])
    scores = jnp.where(allowed, scores, 0.0)
    lower_rows = cum - jnp.log2(dt)
    columns = jnp.transpose(cum)
    lane = lax.broadcasted_iota(jnp.int32, (BLOCK, LANES), 1)
    left = lane < HEAD_DIM
    total = jnp.zeros((BLOCK, LANES), F32)
    for j in range(width // LANES):
        sl = slice(j * LANES, (j + 1) * LANES)
        parts = []
        for h in (2 * j, 2 * j + 1):
            spread = jnp.minimum(columns[:, h : h + 1] - lower_rows[h : h + 1, :], 80.0)
            parts.append((scores * jnp.exp2(spread)).astype(BF16))
        xc = xc_ref[:, sl]
        none = jnp.zeros_like(xc)
        pair = jnp.concatenate([jnp.where(left, xc, none), jnp.where(left, none, xc)], axis=0)
        y = mm(jnp.concatenate(parts, axis=1), pair, ((1,), (0,)))
        xf = xc.astype(F32)
        scaled[:, sl] = (xf * tailw[:, sl]).astype(BF16)
        full = y + cfac[:, sl] * carried[:, sl] + skip_ref[0:1, sl] * xf
        held = full * silu(z_ref[:, sl].astype(F32))
        gated[:, sl] = held
        total = total + held * held
    mean = jnp.sum(total, axis=1, keepdims=True) * (1.0 / width)
    scale = jnp.broadcast_to(lax.rsqrt(mean + 1e-05), (BLOCK, LANES))
    for j in range(width // LANES):
        sl = slice(j * LANES, (j + 1) * LANES)
        out_ref[:, sl] = (gated[:, sl] * scale * gain_ref[0:1, sl]).astype(BF16)

    @pl.when(b < pl.num_programs(1) - 1)
    def _():
        update = mm(b_part, scaled[...], ((0,), (0,)))
        state[...] = cfac[BLOCK - 1 : BLOCK, :] * state[...] + update


def shards(
    x_proj, z_gate, bc_proj, dt_proj, dt_bias, decay_log, skip_gain,
    conv_x, bias_x, conv_bc, bias_bc, norm_gain, seg_lengths,
):
    rows, channels = x_proj.shape
    lookback = conv_x.shape[0] - 1
    heads = dt_proj.shape[1]
    groups = bc_proj.shape[1]
    repeat = heads // groups
    wide = channels // groups
    blocks = rows // BLOCK
    peers = lax.axis_size("seq")
    bc = bc_proj.reshape(rows, groups * 2 * STATE)
    tails = jnp.concatenate([x_proj[rows - TAIL :], bc[rows - TAIL :]], axis=1)
    tails = lax.ppermute(tails, "seq", [(i, i + 1) for i in range(peers - 1)])
    x_tail, bc_tail = tails[:, :channels], tails[:, channels:]

    first_row = lax.axis_index("seq") * rows
    positions = first_row + jnp.arange(-lookback, rows, dtype=jnp.int32)
    segments = segment_of(seg_lengths, positions)
    own = segments[lookback:]
    columns = [(segments[k : k + rows] == own).astype(F32) for k in range(lookback)]
    columns = jnp.stack(columns + [own.astype(F32)] * (8 - lookback), axis=1)
    seg_blocks = own.reshape(blocks, BLOCK)
    before = segments[lookback - 1 :: BLOCK][:blocks]
    same_end = (seg_blocks == seg_blocks[:, -1:]).astype(F32)
    alive = (seg_blocks == before[:, None]).astype(F32)
    alive_end = jnp.broadcast_to(alive[:, -1:], alive.shape)
    lines = jnp.stack([seg_blocks.astype(F32), same_end, alive, alive_end] * 2, axis=1)

    dtp = dt_proj.T
    dtb = dt_bias[:, None]
    dec = decay_log[:, None]
    head_of = jnp.arange(wide)[None, :] // HEAD_DIM
    spread = (head_of == (jnp.arange(2 * repeat) % repeat)[:, None]).astype(BF16)

    def spec(shape, index):
        return pl.BlockSpec(shape, index)

    grid = (groups, blocks)
    tall = lambda w: spec((BLOCK, w), lambda g, b: (b, g))
    flat = lambda n, w: spec((n, w), lambda g, b: (0, g))
    shared = [
        spec((repeat, BLOCK), lambda g, b: (g, b)),
        spec((BLOCK, 8), lambda g, b: (b, 0)),
        spec((1, 8, BLOCK), lambda g, b: (b, 0, 0)),
        spec((repeat, 1), lambda g, b: (g, 0)),
        spec((repeat, 1), lambda g, b: (g, 0)),
    ]
    e_spec = spec((2 * repeat, wide), lambda g, b: (0, 0))
    params = pltpu.CompilerParams(
        dimension_semantics=("arbitrary", "arbitrary"), vmem_limit_bytes=48 << 20
    )
    xc, bcc, summary, decays = pl.pallas_call(
        local_kernel,
        grid=grid,
        in_specs=[
            tall(wide), flat(TAIL, wide), tall(2 * STATE), flat(TAIL, 2 * STATE), *shared,
            flat(lookback + 1, wide), flat(1, wide), flat(lookback + 1, 2 * STATE),
            flat(1, 2 * STATE), e_spec,
        ],
        out_specs=[tall(wide), tall(2 * STATE), flat(STATE, wide), flat(8, wide)],
        out_shape=[
            jax.ShapeDtypeStruct((rows, channels), BF16),
            jax.ShapeDtypeStruct((rows, groups * 2 * STATE), BF16),
            jax.ShapeDtypeStruct((STATE, channels), F32),
            jax.ShapeDtypeStruct((8, channels), F32),
        ],
        scratch_shapes=[
            pltpu.VMEM((BLOCK + 8, wide), F32),
            pltpu.VMEM((BLOCK + 8, 2 * STATE), F32),
            pltpu.VMEM((BLOCK, wide), BF16),
            pltpu.VMEM((BLOCK, wide), F32),
        ],
        compiler_params=params,
        name="local_state",
    )(
        x_proj, x_tail, bc, bc_tail, dtp, columns, lines, dtb, dec,
        conv_x, bias_x[None], conv_bc.reshape(lookback + 1, -1), bias_bc.reshape(1, -1), spread,
    )

    chunks = 16
    incoming = pl.pallas_call(
        functools.partial(chain_kernel, chunks),
        in_specs=[pl.BlockSpec(memory_space=pltpu.VMEM)] * 2,
        out_specs=pl.BlockSpec(memory_space=pltpu.VMEM),
        out_shape=jax.ShapeDtypeStruct((STATE, channels), BF16),
        scratch_shapes=[
            pltpu.VMEM((chunks, STATE, channels // chunks), BF16),
            pltpu.VMEM((chunks, STATE, channels // chunks), BF16),
            pltpu.SemaphoreType.DMA((chunks,)),
            pltpu.SemaphoreType.DMA((chunks,)),
        ],
        compiler_params=pltpu.CompilerParams(collective_id=0, has_side_effects=True),
        name="state_chain",
    )(summary, decays)

    big = pltpu.VMEM((BLOCK, wide), F32)
    return pl.pallas_call(
        output_kernel,
        grid=grid,
        in_specs=[
            tall(wide), tall(2 * STATE), tall(wide), flat(STATE, wide), *shared,
            flat(1, wide), flat(1, wide), e_spec,
        ],
        out_specs=tall(wide),
        out_shape=jax.ShapeDtypeStruct((rows, channels), BF16),
        scratch_shapes=[
            pltpu.VMEM((STATE, wide), F32), big, big, pltpu.VMEM((BLOCK, wide), BF16), big, big,
        ],
        compiler_params=params,
        name="block_outputs",
    )(
        xc, bcc, z_gate, incoming, dtp, columns, lines, dtb, dec,
        jnp.repeat(skip_gain, HEAD_DIM)[None], norm_gain[None], spread,
    )


def solution(mesh):
    return jax.shard_map(
        shards,
        mesh=mesh,
        in_specs=(
            P(("groups", "seq"), "head"),
            P(("groups", "seq"), "head"),
            P(("groups", "seq"), "head", None),
            P(("groups", "seq"), "head"),
            P("head"),
            P("head"),
            P("head"),
            P(None, "head"),
            P("head"),
            P(None, "head", None),
            P("head", None),
            P("head"),
            P("groups"),
        ),
        out_specs=P(("groups", "seq"), "head"),
        check_vma=False,
    )
```

```python
import functools

import jax
import jax.numpy as jnp
from jax import lax
from jax.experimental import pallas as pl
from jax.experimental.pallas import tpu as pltpu
from jax.sharding import PartitionSpec as P

HEAD_DIM = 64
STATE = 128
BLOCK = 128
LANES = 128
TAIL = 16
VMEM_LIMIT = 60 << 20
LOG2E = 1.4426950408889634
MESH = pl.DeviceIdType.MESH
F32 = jnp.float32
BF16 = jnp.bfloat16


def silu_of_half(half):
    return half + half * jnp.tanh(half)


def mm(a, b, dims, precision=None):
    return lax.dot_general(a, b, (dims, ((), ())), precision=precision, preferred_element_type=F32)


def ids_of(starts, positions):
    found = jnp.full(positions.shape, -1, jnp.int32)
    for start in starts:
        found = jnp.where(positions >= start, start, found)
    return found


def id_of(starts, position):
    found = jnp.int32(-1)
    for start in starts:
        found = jnp.where(position >= start, start, found)
    return found


class Spot:
    def __init__(self, seg_ref, block):
        rows = pl.num_programs(0) * BLOCK
        at = lax.axis_index("seq") * rows + block * BLOCK
        starts = [jnp.int32(0)]
        for j in range(seg_ref.shape[0] - 1):
            starts.append(starts[-1] + seg_ref[j])
        self.tall = at + lax.broadcasted_iota(jnp.int32, (BLOCK, LANES), 0)
        self.tall_id = ids_of(starts, self.tall)
        row = at + lax.broadcasted_iota(jnp.int32, (1, LANES), 1)
        self.row_id = ids_of(starts, row)
        before = id_of(starts, at - 1)
        end = id_of(starts, at + BLOCK - 1)
        self.same_end = (self.row_id == end).astype(F32)
        self.alive = (self.row_id == before).astype(F32)
        self.alive_end = (end == before).astype(F32)


def column(row):
    n = row.shape[1]
    i = lax.broadcasted_iota(jnp.int32, (n, n), 0)
    j = lax.broadcasted_iota(jnp.int32, (n, n), 1)
    return jnp.sum(jnp.where(i == j, row, 0.0), axis=1, keepdims=True)


def steps_of(dtp_ref, dtb_ref, dec_ref):
    raw = dtp_ref[...].astype(F32) + column(dtb_ref[...])
    dt = jnp.maximum(raw, 0.0) + jnp.log1p(jnp.exp(-jnp.abs(raw)))
    la = (-LOG2E * column(jnp.exp(dec_ref[...]))) * dt
    s = lax.broadcasted_iota(jnp.int32, (BLOCK, BLOCK), 0)
    t = lax.broadcasted_iota(jnp.int32, (BLOCK, BLOCK), 1)
    upper = (s <= t).astype(F32)
    return dt, mm(la, upper, ((1,), (0,)), lax.Precision.HIGHEST)


def fill_spread(e_ref):
    twice, wide = e_ref.shape
    row = lax.broadcasted_iota(jnp.int32, (twice, wide), 0)
    lane = lax.broadcasted_iota(jnp.int32, (twice, wide), 1)
    e_ref[...] = (lane // HEAD_DIM == row % (twice // 2)).astype(F32).astype(BF16)


def expand(value, e_ref):
    hi = value.astype(BF16)
    lo = (value - hi.astype(F32)).astype(BF16)
    return mm(jnp.concatenate([hi, lo], axis=0), e_ref[...], ((0,), (0,)))


def conv_tile(dst, src, halo, sl, weights, bias, masks):
    own = src[:, sl].astype(F32)
    halo[8 : BLOCK + 8, sl] = own
    total = 0.5 * bias + (0.5 * weights[3]) * own
    for k in range(3):
        total = total + (0.5 * weights[k]) * (halo[5 + k : 5 + k + BLOCK, sl] * masks[k])
    dst[:, sl] = silu_of_half(total).astype(BF16)


def tiles(start, width):
    return [slice(start + j, start + j + LANES) for j in range(0, width, LANES)]


def local_kernel(
    groups, seg_ref, x_ref, bc_ref, tail_ref, dtp_ref, dtb_ref, dec_ref,
    wx_ref, bx_ref, wbc_ref, bbc_ref,
    xc_ref, bcc_ref, s_ref, d_ref, xhalo, bhalo, scaled, e_ref,
):
    b = pl.program_id(0)
    channels = x_ref.shape[1]
    wide = channels // groups
    repeat = dtp_ref.shape[0] // groups

    @pl.when(b == 0)
    def _():
        fill_spread(e_ref)
        s_ref[...] = jnp.zeros(s_ref.shape, F32)
        d_ref[...] = jnp.ones(d_ref.shape, F32)
        xhalo[0:8, :] = tail_ref[TAIL - 8 : TAIL, 0:channels].astype(F32)
        bhalo[0:8, :] = tail_ref[TAIL - 8 : TAIL, channels:].astype(F32)

    @pl.when(b > 0)
    def _():
        xhalo[0:8, :] = xhalo[BLOCK : BLOCK + 8, :]
        bhalo[0:8, :] = bhalo[BLOCK : BLOCK + 8, :]

    spot = Spot(seg_ref, b)
    within = spot.tall - spot.tall_id
    masks = [(within >= 3 - k).astype(F32) for k in range(3)]
    dt, cum = steps_of(dtp_ref, dtb_ref, dec_ref)
    last = cum[:, BLOCK - 1 : BLOCK]
    tail_weight = jnp.exp2(last - cum) * dt * spot.same_end
    end_decay = jnp.exp2(jnp.broadcast_to(last, cum.shape)) * spot.alive_end
    for g in range(groups):
        heads = slice(g * repeat, (g + 1) * repeat)
        lanes = slice(g * wide, (g + 1) * wide)
        for j, sl in enumerate(tiles(g * 2 * STATE, 2 * STATE)):
            part = slice(j * LANES, (j + 1) * LANES)
            weights = [wbc_ref[k, g : g + 1, part] for k in range(4)]
            conv_tile(bcc_ref, bc_ref, bhalo, sl, weights, bbc_ref[g : g + 1, part], masks)
        tailw = expand(tail_weight[heads], e_ref)
        decay = expand(end_decay[heads], e_ref)[0:8]
        for j, sl in enumerate(tiles(g * wide, wide)):
            weights = [wx_ref[k : k + 1, sl] for k in range(4)]
            conv_tile(xc_ref, x_ref, xhalo, sl, weights, bx_ref[0:1, sl], masks)
            part = slice(j * LANES, (j + 1) * LANES)
            scaled[:, sl] = (xc_ref[:, sl].astype(F32) * tailw[:, part]).astype(BF16)
        b_part = bcc_ref[:, g * 2 * STATE : g * 2 * STATE + STATE]
        update = mm(b_part, scaled[:, lanes], ((0,), (0,)))
        s_ref[:, lanes] = decay[0:1] * s_ref[:, lanes] + update
        d_ref[:, lanes] = decay * d_ref[:, lanes]


def chain_kernel(
    chunks, s_ref, d_ref, in_ref, give, theirs, their_d, total, both_d, sendbuf, recvbuf, back,
    backed, give_sem, theirs_sem, send_sem, recv_sem, back_sem, backed_sem, d_sem,
):
    peers = lax.axis_size("seq")
    me = lax.axis_index("seq")
    core, link, links = lax.rem(me, 2), me // 2, peers // 2
    low = core == 0
    half = s_ref.shape[1] // 2
    width = half // chunks
    partner = me + 1 - 2 * core
    following = lax.rem(me + 2, peers)
    barrier = pltpu.get_barrier_semaphore()
    for peer in (partner, following, lax.rem(me + peers - 2, peers)):
        pl.semaphore_signal(barrier, inc=1, device_id={"seq": peer}, device_id_type=MESH)
    pl.semaphore_wait(barrier, 3)

    def piece(which, k):
        return pl.ds(pl.multiple_of(which * half + k * width, LANES), width)

    def copy(src, dst, sem, sem2, peer):
        return pltpu.make_async_remote_copy(
            src_ref=src, dst_ref=dst, send_sem=sem, recv_sem=sem2,
            device_id={"seq": peer}, device_id_type=MESH,
        )

    def give_copy(k):
        return copy(give.at[k], theirs.at[k], give_sem.at[k], theirs_sem.at[k], partner)

    def send_copy(k):
        return copy(sendbuf.at[k], recvbuf.at[k], send_sem.at[k], recv_sem.at[k], following)

    def back_copy(k):
        return copy(back.at[k], backed.at[k], back_sem.at[k], backed_sem.at[k], partner)

    d_copy = copy(d_ref, their_d, d_sem.at[0], d_sem.at[1], partner)
    d_copy.start()
    for k in range(chunks):
        give[k] = s_ref[:, piece(1 - core, k)].astype(BF16)
        give_copy(k).start()
    d_copy.wait()
    for k in range(chunks):
        give_copy(k).wait()
        mine, other = s_ref[:, piece(core, k)], theirs[k].astype(F32)
        d_mine, d_other = d_ref[0:1, piece(core, k)], their_d[0:1, piece(core, k)]
        d_late = jnp.where(low, d_other, d_mine)
        total[k] = d_late * jnp.where(low, mine, other) + jnp.where(low, other, mine)
        both_d[k] = jnp.broadcast_to(d_mine * d_other, (8, width))

        @pl.when(link == 0)
        def _():
            sendbuf[k] = total[k].astype(BF16)
            send_copy(k).start()

    for k in range(chunks):

        @pl.when(link == 0)
        def _():
            recvbuf[k] = jnp.zeros((STATE, width), BF16)

        @pl.when(link > 0)
        def _():
            send_copy(k).wait_recv()

        arrived = recvbuf[k].astype(F32)

        @pl.when((link > 0) & (link < links - 1))
        def _():
            sendbuf[k] = (both_d[k, 0:1] * arrived + total[k]).astype(BF16)
            send_copy(k).start()

        mine, other = s_ref[:, piece(core, k)], theirs[k].astype(F32)
        d_mine, d_other = d_ref[0:1, piece(core, k)], their_d[0:1, piece(core, k)]
        passed = jnp.where(low, d_mine, d_other) * arrived + jnp.where(low, mine, other)
        in_ref[:, piece(core, k)] = jnp.where(low, arrived, passed).astype(BF16)
        back[k] = jnp.where(low, passed, arrived).astype(BF16)
        back_copy(k).start()
    for k in range(chunks):
        back_copy(k).wait()
        in_ref[:, piece(1 - core, k)] = backed[k]

        @pl.when(link < links - 1)
        def _():
            send_copy(k).wait_send()


def output_kernel(
    groups, seg_ref, xc_ref, bcc_ref, z_ref, in_ref, dtp_ref, dtb_ref, dec_ref, skip_ref, gain_ref,
    out_ref, state, cfac, scaled, carried, gated, skip_row, e_ref,
):
    b = pl.program_id(0)
    channels = xc_ref.shape[1]
    wide = channels // groups
    repeat = dtp_ref.shape[0] // groups

    @pl.when(b == 0)
    def _():
        fill_spread(e_ref)
        state[...] = in_ref[...].astype(F32)
        skip = jnp.broadcast_to(column(skip_ref[...]), (groups * repeat, LANES))
        for g in range(groups):
            rows = skip[g * repeat : (g + 1) * repeat]
            skip_row[:, g * wide : (g + 1) * wide] = expand(rows, e_ref)[0:8]

    spot = Spot(seg_ref, b)
    dt, cum = steps_of(dtp_ref, dtb_ref, dec_ref)
    carry_weight = jnp.exp2(cum) * spot.alive
    last = cum[:, BLOCK - 1 : BLOCK]
    tail_weight = jnp.exp2(last - cum) * dt * spot.same_end
    lower_rows = cum - jnp.log2(dt)
    columns = jnp.transpose(cum)
    t = lax.broadcasted_iota(jnp.int32, (BLOCK, BLOCK), 0)
    s = lax.broadcasted_iota(jnp.int32, (BLOCK, BLOCK), 1)
    allowed = (s <= t) & (spot.tall_id == spot.row_id)
    lane = lax.broadcasted_iota(jnp.int32, (BLOCK, LANES), 1)
    left = lane < HEAD_DIM
    for g in range(groups):
        heads = slice(g * repeat, (g + 1) * repeat)
        lanes = slice(g * wide, (g + 1) * wide)
        cfac[:, lanes] = expand(carry_weight[heads], e_ref)
        tailw = expand(tail_weight[heads], e_ref)
        b_part = bcc_ref[:, g * 2 * STATE : g * 2 * STATE + STATE]
        c_part = bcc_ref[:, g * 2 * STATE + STATE : (g + 1) * 2 * STATE]
        carried[:, lanes] = mm(c_part, state[:, lanes].astype(BF16), ((1,), (0,)))
        scores = jnp.where(allowed, mm(c_part, b_part, ((1,), (1,))), 0.0)
        squares = jnp.zeros((BLOCK, LANES), F32)
        for j, sl in enumerate(tiles(g * wide, wide)):
            parts = []
            for h in (g * repeat + 2 * j, g * repeat + 2 * j + 1):
                spread = jnp.minimum(columns[:, h : h + 1] - lower_rows[h : h + 1, :], 80.0)
                parts.append((scores * jnp.exp2(spread)).astype(BF16))
            xc = xc_ref[:, sl]
            none = jnp.zeros_like(xc)
            pair = jnp.concatenate([jnp.where(left, xc, none), jnp.where(left, none, xc)], axis=0)
            y = mm(jnp.concatenate(parts, axis=1), pair, ((1,), (0,)))
            xf = xc.astype(F32)
            scaled[:, sl] = (xf * tailw[:, j * LANES : (j + 1) * LANES]).astype(BF16)
            full = y + cfac[:, sl] * carried[:, sl] + skip_row[0:1, sl] * xf
            held = full * silu_of_half(0.5 * z_ref[:, sl].astype(F32))
            gated[:, sl] = held
            squares = squares + held * held
        mean = jnp.sum(squares, axis=1, keepdims=True) * (1.0 / wide)
        scale = jnp.broadcast_to(lax.rsqrt(mean + 1e-05), (BLOCK, LANES))
        for sl in tiles(g * wide, wide):
            out_ref[:, sl] = (gated[:, sl] * scale * gain_ref[0:1, sl]).astype(BF16)
        update = mm(b_part, scaled[:, lanes], ((0,), (0,)))
        state[:, lanes] = cfac[BLOCK - 1 : BLOCK, lanes] * state[:, lanes] + update


def shards(
    x_proj, z_gate, bc_proj, dt_proj, dt_bias, decay_log, skip_gain,
    conv_x, bias_x, conv_bc, bias_bc, norm_gain, seg_lengths,
):
    rows, channels = x_proj.shape
    lookback = conv_x.shape[0] - 1
    heads = dt_proj.shape[1]
    groups = bc_proj.shape[1]
    repeat = heads // groups
    wide = channels // groups
    blocks = rows // BLOCK
    peers = lax.axis_size("seq")
    bc = bc_proj.reshape(rows, groups * 2 * STATE)
    tails = jnp.concatenate([x_proj[rows - TAIL :], bc[rows - TAIL :]], axis=1)
    tails = lax.ppermute(tails, "seq", [(i, i + 1) for i in range(peers - 1)])
    dtp = dt_proj.T
    tall = lambda w: pl.BlockSpec((BLOCK, w), lambda b: (b, 0))
    whole = lambda *shape: pl.BlockSpec(shape, lambda b: (0,) * len(shape))
    lengths = pl.BlockSpec(memory_space=pltpu.SMEM)
    scalars = [pl.BlockSpec((heads, BLOCK), lambda b: (0, b)), whole(1, heads), whole(1, heads)]
    params = pltpu.CompilerParams(
        dimension_semantics=("arbitrary",), vmem_limit_bytes=VMEM_LIMIT
    )
    pairs = groups * 2 * STATE
    xc, bcc, summary, decays = pl.pallas_call(
        functools.partial(local_kernel, groups),
        grid=(blocks,),
        in_specs=[
            lengths, tall(channels), tall(pairs), whole(TAIL, channels + pairs), *scalars,
            whole(lookback + 1, channels), whole(1, channels),
            whole(lookback + 1, groups, 2 * STATE), whole(groups, 2 * STATE),
        ],
        out_specs=[tall(channels), tall(pairs), whole(STATE, channels), whole(8, channels)],
        out_shape=[
            jax.ShapeDtypeStruct((rows, channels), BF16),
            jax.ShapeDtypeStruct((rows, pairs), BF16),
            jax.ShapeDtypeStruct((STATE, channels), F32),
            jax.ShapeDtypeStruct((8, channels), F32),
        ],
        scratch_shapes=[
            pltpu.VMEM((BLOCK + 8, channels), F32),
            pltpu.VMEM((BLOCK + 8, pairs), F32),
            pltpu.VMEM((BLOCK, channels), BF16),
            pltpu.VMEM((2 * repeat, wide), BF16),
        ],
        compiler_params=params,
        name="local_state",
    )(
        seg_lengths, x_proj, bc, tails, dtp, dt_bias[None], decay_log[None],
        conv_x, bias_x[None], conv_bc, bias_bc,
    )

    chunks = 16
    width = channels // 2 // chunks
    pieces = pltpu.VMEM((chunks, STATE, width), BF16)
    sems = pltpu.SemaphoreType.DMA((chunks,))
    incoming = pl.pallas_call(
        functools.partial(chain_kernel, chunks),
        in_specs=[pl.BlockSpec(memory_space=pltpu.VMEM)] * 2,
        out_specs=pl.BlockSpec(memory_space=pltpu.VMEM),
        out_shape=jax.ShapeDtypeStruct((STATE, channels), BF16),
        scratch_shapes=[
            pieces, pieces, pltpu.VMEM((8, channels), F32),
            pltpu.VMEM((chunks, STATE, width), F32), pltpu.VMEM((chunks, 8, width), F32),
            pieces, pieces, pieces, pieces,
            sems, sems, sems, sems, sems, sems, pltpu.SemaphoreType.DMA((2,)),
        ],
        compiler_params=pltpu.CompilerParams(
            collective_id=0, has_side_effects=True, vmem_limit_bytes=VMEM_LIMIT
        ),
        name="state_chain",
    )(summary, decays)

    big = pltpu.VMEM((BLOCK, channels), F32)
    return pl.pallas_call(
        functools.partial(output_kernel, groups),
        grid=(blocks,),
        in_specs=[
            lengths, tall(channels), tall(pairs), tall(channels), whole(STATE, channels), *scalars,
            whole(1, heads), whole(1, channels),
        ],
        out_specs=tall(channels),
        out_shape=jax.ShapeDtypeStruct((rows, channels), BF16),
        scratch_shapes=[
            pltpu.VMEM((STATE, channels), F32), big, pltpu.VMEM((BLOCK, channels), BF16), big, big,
            pltpu.VMEM((8, channels), F32), pltpu.VMEM((2 * repeat, wide), BF16),
        ],
        compiler_params=params,
        name="block_outputs",
    )(
        seg_lengths, xc, bcc, z_gate, incoming, dtp, dt_bias[None], decay_log[None],
        skip_gain[None], norm_gain[None],
    )


def solution(mesh):
    return jax.shard_map(
        shards,
        mesh=mesh,
        in_specs=(
            P(("groups", "seq"), "head"),
            P(("groups", "seq"), "head"),
            P(("groups", "seq"), "head", None),
            P(("groups", "seq"), "head"),
            P("head"),
            P("head"),
            P("head"),
            P(None, "head"),
            P("head"),
            P(None, "head", None),
            P("head", None),
            P("head"),
            P("groups"),
        ),
        out_specs=P(("groups", "seq"), "head"),
        check_vma=False,
    )
```

```python
import functools

import jax
import jax.numpy as jnp
from jax import lax
from jax.experimental import pallas as pl
from jax.experimental.pallas import tpu as pltpu
from jax.sharding import PartitionSpec as P

HEAD_DIM = 64
STATE = 128
BLOCK = 128
LANES = 128
TAIL = 16
VMEM_LIMIT = 60 << 20
LOG2E = 1.4426950408889634
MESH = pl.DeviceIdType.MESH
F32 = jnp.float32
BF16 = jnp.bfloat16


def silu_of_half(half):
    return half + half * jnp.tanh(half)


def mm(a, b, dims, precision=None):
    return lax.dot_general(a, b, (dims, ((), ())), precision=precision, preferred_element_type=F32)


def ids_of(starts, positions):
    found = jnp.full(positions.shape, -1, jnp.int32)
    for start in starts:
        found = jnp.where(positions >= start, start, found)
    return found


def id_of(starts, position):
    found = jnp.int32(-1)
    for start in starts:
        found = jnp.where(position >= start, start, found)
    return found


class Spot:
    def __init__(self, seg_ref, block):
        rows = pl.num_programs(0) * BLOCK
        at = lax.axis_index("seq") * rows + block * BLOCK
        starts = [jnp.int32(0)]
        for j in range(seg_ref.shape[0] - 1):
            starts.append(starts[-1] + seg_ref[j])
        self.tall = at + lax.broadcasted_iota(jnp.int32, (BLOCK, LANES), 0)
        self.tall_id = ids_of(starts, self.tall)
        row = at + lax.broadcasted_iota(jnp.int32, (1, LANES), 1)
        self.row_id = ids_of(starts, row)
        before = id_of(starts, at - 1)
        end = id_of(starts, at + BLOCK - 1)
        self.same_end = (self.row_id == end).astype(F32)
        self.alive = (self.row_id == before).astype(F32)
        self.alive_end = (end == before).astype(F32)


def column(row):
    n = row.shape[1]
    i = lax.broadcasted_iota(jnp.int32, (n, n), 0)
    j = lax.broadcasted_iota(jnp.int32, (n, n), 1)
    return jnp.sum(jnp.where(i == j, row, 0.0), axis=1, keepdims=True)


def steps_of(dtp_ref, dtb_ref, dec_ref):
    raw = dtp_ref[...].astype(F32) + column(dtb_ref[...])
    dt = jnp.maximum(raw, 0.0) + jnp.log1p(jnp.exp(-jnp.abs(raw)))
    la = (-LOG2E * column(jnp.exp(dec_ref[...]))) * dt
    s = lax.broadcasted_iota(jnp.int32, (BLOCK, BLOCK), 0)
    t = lax.broadcasted_iota(jnp.int32, (BLOCK, BLOCK), 1)
    upper = (s <= t).astype(F32)
    return dt, mm(la, upper, ((1,), (0,)), lax.Precision.HIGHEST)


def fill_spread(e_ref):
    twice, wide = e_ref.shape
    row = lax.broadcasted_iota(jnp.int32, (twice, wide), 0)
    lane = lax.broadcasted_iota(jnp.int32, (twice, wide), 1)
    e_ref[...] = (lane // HEAD_DIM == row % (twice // 2)).astype(F32).astype(BF16)


def expand(value, e_ref):
    hi = value.astype(BF16)
    lo = (value - hi.astype(F32)).astype(BF16)
    return mm(jnp.concatenate([hi, lo], axis=0), e_ref[...], ((0,), (0,)))


def shift_matrix(within):
    t = lax.broadcasted_iota(jnp.int32, (BLOCK, TAIL + BLOCK), 0)
    i = lax.broadcasted_iota(jnp.int32, (BLOCK, TAIL + BLOCK), 1)
    steps = [((i == t + (TAIL - 3 + k)) & (within[:, 0:1] >= 3 - k)).astype(F32) for k in range(3)]
    return jnp.concatenate(steps, axis=0).astype(BF16)


def conv_tile(dst, halo, shift, cols, out, weights, bias):
    src = halo[:, cols]
    past = mm(shift, src, ((1,), (0,)))
    own = src[TAIL:, :].astype(F32)
    half = 0.5 * bias + (0.5 * weights[3]) * own
    for k in range(3):
        half = half + (0.5 * weights[k]) * past[k * BLOCK : (k + 1) * BLOCK]
    value = silu_of_half(half).astype(BF16)
    dst[:, out] = value
    return value


def tiles(start, width):
    return [slice(start + j, start + j + LANES) for j in range(0, width, LANES)]


def local_kernel(
    groups, seg_ref, x_ref, bc_ref, tail_ref, dtp_ref, dtb_ref, dec_ref,
    wx_ref, bx_ref, wbc_ref, bbc_ref,
    xc_ref, bcc_ref, s_ref, d_ref, xhalo, bhalo, scaled, e_ref,
):
    b = pl.program_id(0)
    channels = x_ref.shape[1]
    wide = channels // groups
    repeat = dtp_ref.shape[0] // groups

    @pl.when(b == 0)
    def _():
        fill_spread(e_ref)
        s_ref[...] = jnp.zeros(s_ref.shape, F32)
        d_ref[...] = jnp.ones(d_ref.shape, F32)
        xhalo[0:TAIL, :] = tail_ref[:, 0:channels]
        bhalo[0:TAIL, :] = tail_ref[:, channels:]

    @pl.when(b > 0)
    def _():
        xhalo[0:TAIL, :] = xhalo[BLOCK : BLOCK + TAIL, :]
        bhalo[0:TAIL, :] = bhalo[BLOCK : BLOCK + TAIL, :]

    xhalo[TAIL:, :] = x_ref[...]
    bhalo[TAIL:, :] = bc_ref[...]
    spot = Spot(seg_ref, b)
    shift = shift_matrix(spot.tall - spot.tall_id)
    dt, cum = steps_of(dtp_ref, dtb_ref, dec_ref)
    last = cum[:, BLOCK - 1 : BLOCK]
    tail_weight = jnp.exp2(last - cum) * dt * spot.same_end
    end_decay = jnp.exp2(jnp.broadcast_to(last, cum.shape)) * spot.alive_end
    for g in range(groups):
        heads = slice(g * repeat, (g + 1) * repeat)
        lanes = slice(g * wide, (g + 1) * wide)
        sl = slice(g * 2 * STATE, (g + 1) * 2 * STATE)
        weights = [wbc_ref[k, g : g + 1, :] for k in range(4)]
        conv_tile(bcc_ref, bhalo, shift, sl, sl, weights, bbc_ref[g : g + 1, :])
        tailw = expand(tail_weight[heads], e_ref)
        decay = expand(end_decay[heads], e_ref)[0:8]
        for j in range(0, wide, 2 * LANES):
            sl = slice(g * wide + j, g * wide + j + 2 * LANES)
            weights = [wx_ref[k : k + 1, sl] for k in range(4)]
            value = conv_tile(xc_ref, xhalo, shift, sl, sl, weights, bx_ref[0:1, sl])
            scaled[:, sl] = (value.astype(F32) * tailw[:, j : j + 2 * LANES]).astype(BF16)
        b_part = bcc_ref[:, g * 2 * STATE : g * 2 * STATE + STATE]
        update = mm(b_part, scaled[:, lanes], ((0,), (0,)))
        s_ref[:, lanes] = decay[0:1] * s_ref[:, lanes] + update
        d_ref[:, lanes] = decay * d_ref[:, lanes]


def chain_kernel(
    chunks, s_ref, d_ref, in_ref, give1, take1, give2, take2, total1, total2, sent, arrive,
    back2, home2, back1, home1, hold_d1, both_d1, hold_d2, both_d2, sem1, sem2, sem3, sem4, sem5, dsem,
):
    peers = lax.axis_size("seq")
    me = lax.axis_index("seq")
    core, pair, link, links = lax.rem(me, 2), lax.rem(me // 2, 2), me // 4, peers // 4
    low1, low2 = core == 0, pair == 0
    half = s_ref.shape[1] // 2
    quarter = half // 2
    width = quarter // chunks
    near, far = me + 1 - 2 * core, me + 2 - 4 * pair
    following = lax.rem(me + 4, peers)
    barrier = pltpu.get_barrier_semaphore()
    for peer in (near, far, following, lax.rem(me + peers - 4, peers)):
        pl.semaphore_signal(barrier, inc=1, device_id={"seq": peer}, device_id_type=MESH)
    pl.semaphore_wait(barrier, 4)

    def lanes(which, k):
        return pl.ds(pl.multiple_of(which * half + k * width, LANES), width)

    def inner(k):
        return pl.ds(pl.multiple_of(k * width, LANES), width)

    def copy(src, dst, sems, peer):
        return pltpu.make_async_remote_copy(
            src_ref=src, dst_ref=dst, send_sem=sems.at[0], recv_sem=sems.at[1],
            device_id={"seq": peer}, device_id_type=MESH,
        )

    def copy1(k):
        return copy(give1.at[k], take1.at[k], sem1.at[k], near)

    def copy2(k):
        return copy(give2.at[k], take2.at[k], sem2.at[k], far)

    def copy3(k):
        return copy(sent.at[k], arrive.at[k], sem3.at[k], following)

    def copy4(k):
        return copy(back2.at[k], home2.at[k], sem4.at[k], far)

    def copy5(k):
        return copy(back1.at[k], home1.at[k], sem5.at[k], near)

    def half_lanes(which):
        return pl.ds(pl.multiple_of(which * half, LANES), half)

    def quarter_lanes(which):
        return pl.ds(pl.multiple_of(which * quarter, LANES), quarter)

    dcopy1 = copy(d_ref.at[:, half_lanes(1 - core)], hold_d1, dsem.at[0], near)
    dcopy2 = copy(both_d1.at[:, quarter_lanes(1 - pair)], hold_d2, dsem.at[1], far)
    dcopy1.start()
    theirs, ours = (1 - pair) * chunks, pair * chunks
    order = [theirs + k for k in range(chunks)] + [ours + k for k in range(chunks)]
    for k in order:
        give1[k] = s_ref[:, lanes(1 - core, k)].astype(BF16)
        copy1(k).start()
    dcopy1.wait()
    both_d1[...] = d_ref[:, half_lanes(core)] * hold_d1[...]
    dcopy2.start()

    def merge1(k):
        copy1(k).wait()
        mine, other = s_ref[:, lanes(core, k)], take1[k].astype(F32)
        d_late = jnp.where(low1, hold_d1[0:1, inner(k)], d_ref[0:1, lanes(core, k)])
        return d_late * jnp.where(low1, mine, other) + jnp.where(low1, other, mine)

    for k in range(chunks):
        give2[k] = merge1(theirs + k).astype(BF16)
        copy2(k).start()
    for k in range(chunks):
        total1[k] = merge1(ours + k)
    dcopy2.wait()
    both_d2[...] = both_d1[:, quarter_lanes(pair)] * hold_d2[...]

    def part(k):
        return slice(k * width, (k + 1) * width)

    for k in range(chunks):
        copy2(k).wait()
        mine, other = total1[k], take2[k].astype(F32)
        d_late = jnp.where(low2, hold_d2[0:1, part(k)], both_d1[0:1, inner(ours + k)])
        total2[k] = d_late * jnp.where(low2, mine, other) + jnp.where(low2, other, mine)

        @pl.when(link == 0)
        def _():
            sent[k] = total2[k].astype(BF16)
            copy3(k).start()

    def hand_over(k, into):
        mine, other = s_ref[:, lanes(core, k)], take1[k].astype(F32)
        d_early = jnp.where(low1, d_ref[0:1, lanes(core, k)], hold_d1[0:1, inner(k)])
        passed = d_early * into + jnp.where(low1, mine, other)
        in_ref[:, lanes(core, k)] = jnp.where(low1, into, passed).astype(BF16)
        back1[k] = jnp.where(low1, passed, into).astype(BF16)
        copy5(k).start()

    for k in range(chunks):

        @pl.when(link == 0)
        def _():
            arrive[k] = jnp.zeros((STATE, width), BF16)

        @pl.when(link > 0)
        def _():
            copy3(k).wait_recv()

        into = arrive[k].astype(F32)

        @pl.when((link > 0) & (link < links - 1))
        def _():
            sent[k] = (both_d2[0:1, part(k)] * into + total2[k]).astype(BF16)
            copy3(k).start()

        mine, other = total1[k], take2[k].astype(F32)
        d_early = jnp.where(low2, both_d1[0:1, inner(ours + k)], hold_d2[0:1, part(k)])
        passed = d_early * into + jnp.where(low2, mine, other)
        back2[k] = jnp.where(low2, passed, into).astype(BF16)
        copy4(k).start()
        hand_over(ours + k, jnp.where(low2, into, passed))
    for k in range(chunks):
        copy4(k).wait()
        hand_over(theirs + k, home2[k].astype(F32))
    for k in order[chunks:] + order[:chunks]:
        copy5(k).wait()
        in_ref[:, lanes(1 - core, k)] = home1[k]
    for k in range(chunks):

        @pl.when(link < links - 1)
        def _():
            copy3(k).wait_send()


def output_kernel(
    groups, seg_ref, xc_ref, bcc_ref, z_ref, in_ref, dtp_ref, dtb_ref, dec_ref, skip_ref, gain_ref,
    out_ref, state, cfac, scaled, carried, gated, skip_row, e_ref,
):
    b = pl.program_id(0)
    channels = xc_ref.shape[1]
    wide = channels // groups
    repeat = dtp_ref.shape[0] // groups

    @pl.when(b == 0)
    def _():
        fill_spread(e_ref)
        state[...] = in_ref[...].astype(F32)
        skip = jnp.broadcast_to(column(skip_ref[...]), (groups * repeat, LANES))
        for g in range(groups):
            rows = skip[g * repeat : (g + 1) * repeat]
            skip_row[:, g * wide : (g + 1) * wide] = expand(rows, e_ref)[0:8]

    spot = Spot(seg_ref, b)
    dt, cum = steps_of(dtp_ref, dtb_ref, dec_ref)
    carry_weight = jnp.exp2(cum) * spot.alive
    last = cum[:, BLOCK - 1 : BLOCK]
    tail_weight = jnp.exp2(last - cum) * dt * spot.same_end
    lower_rows = cum - jnp.log2(dt)
    columns = jnp.transpose(cum)
    t = lax.broadcasted_iota(jnp.int32, (BLOCK, BLOCK), 0)
    s = lax.broadcasted_iota(jnp.int32, (BLOCK, BLOCK), 1)
    allowed = (s <= t) & (spot.tall_id == spot.row_id)
    lane = lax.broadcasted_iota(jnp.int32, (BLOCK, LANES), 1)
    left = lane < HEAD_DIM
    for g in range(groups):
        heads = slice(g * repeat, (g + 1) * repeat)
        lanes = slice(g * wide, (g + 1) * wide)
        cfac[:, lanes] = expand(carry_weight[heads], e_ref)
        tailw = expand(tail_weight[heads], e_ref)
        b_part = bcc_ref[:, g * 2 * STATE : g * 2 * STATE + STATE]
        c_part = bcc_ref[:, g * 2 * STATE + STATE : (g + 1) * 2 * STATE]
        carried[:, lanes] = mm(c_part, state[:, lanes].astype(BF16), ((1,), (0,)))
        scores = jnp.where(allowed, mm(c_part, b_part, ((1,), (1,))), 0.0)
        squares = jnp.zeros((BLOCK, LANES), F32)
        for j, sl in enumerate(tiles(g * wide, wide)):
            parts = []
            for h in (g * repeat + 2 * j, g * repeat + 2 * j + 1):
                spread = jnp.minimum(columns[:, h : h + 1] - lower_rows[h : h + 1, :], 80.0)
                parts.append((scores * jnp.exp2(spread)).astype(BF16))
            xc = xc_ref[:, sl]
            none = jnp.zeros_like(xc)
            pair = jnp.concatenate([jnp.where(left, xc, none), jnp.where(left, none, xc)], axis=0)
            y = mm(jnp.concatenate(parts, axis=1), pair, ((1,), (0,)))
            xf = xc.astype(F32)
            scaled[:, sl] = (xf * tailw[:, j * LANES : (j + 1) * LANES]).astype(BF16)
            full = y + cfac[:, sl] * carried[:, sl] + skip_row[0:1, sl] * xf
            held = full * silu_of_half(0.5 * z_ref[:, sl].astype(F32))
            gated[:, sl] = held
            squares = squares + held * held
        mean = jnp.sum(squares, axis=1, keepdims=True) * (1.0 / wide)
        scale = jnp.broadcast_to(lax.rsqrt(mean + 1e-05), (BLOCK, LANES))
        for sl in tiles(g * wide, wide):
            out_ref[:, sl] = (gated[:, sl] * scale * gain_ref[0:1, sl]).astype(BF16)
        update = mm(b_part, scaled[:, lanes], ((0,), (0,)))
        state[:, lanes] = cfac[BLOCK - 1 : BLOCK, lanes] * state[:, lanes] + update


def shards(
    x_proj, z_gate, bc_proj, dt_proj, dt_bias, decay_log, skip_gain,
    conv_x, bias_x, conv_bc, bias_bc, norm_gain, seg_lengths,
):
    rows, channels = x_proj.shape
    lookback = conv_x.shape[0] - 1
    heads = dt_proj.shape[1]
    groups = bc_proj.shape[1]
    repeat = heads // groups
    wide = channels // groups
    blocks = rows // BLOCK
    peers = lax.axis_size("seq")
    bc = bc_proj.reshape(rows, groups * 2 * STATE)
    tails = jnp.concatenate([x_proj[rows - TAIL :], bc[rows - TAIL :]], axis=1)
    tails = lax.ppermute(tails, "seq", [(i, i + 1) for i in range(peers - 1)])
    dtp = dt_proj.T
    tall = lambda w: pl.BlockSpec((BLOCK, w), lambda b: (b, 0))
    whole = lambda *shape: pl.BlockSpec(shape, lambda b: (0,) * len(shape))
    lengths = pl.BlockSpec(memory_space=pltpu.SMEM)
    scalars = [pl.BlockSpec((heads, BLOCK), lambda b: (0, b)), whole(1, heads), whole(1, heads)]
    params = pltpu.CompilerParams(
        dimension_semantics=("arbitrary",), vmem_limit_bytes=VMEM_LIMIT
    )
    pairs = groups * 2 * STATE
    xc, bcc, summary, decays = pl.pallas_call(
        functools.partial(local_kernel, groups),
        grid=(blocks,),
        in_specs=[
            lengths, tall(channels), tall(pairs), whole(TAIL, channels + pairs), *scalars,
            whole(lookback + 1, channels), whole(1, channels),
            whole(lookback + 1, groups, 2 * STATE), whole(groups, 2 * STATE),
        ],
        out_specs=[tall(channels), tall(pairs), whole(STATE, channels), whole(8, channels)],
        out_shape=[
            jax.ShapeDtypeStruct((rows, channels), BF16),
            jax.ShapeDtypeStruct((rows, pairs), BF16),
            jax.ShapeDtypeStruct((STATE, channels), F32),
            jax.ShapeDtypeStruct((8, channels), F32),
        ],
        scratch_shapes=[
            pltpu.VMEM((TAIL + BLOCK, channels), BF16),
            pltpu.VMEM((TAIL + BLOCK, pairs), BF16),
            pltpu.VMEM((BLOCK, channels), BF16),
            pltpu.VMEM((2 * repeat, wide), BF16),
        ],
        compiler_params=params,
        name="local_state",
    )(
        seg_lengths, x_proj, bc, tails, dtp, dt_bias[None], decay_log[None],
        conv_x, bias_x[None], conv_bc, bias_bc,
    )

    chunks = max(1, min(8, channels // 4 // LANES))
    quarter = channels // 4
    width = quarter // chunks
    ones, twos = (pltpu.VMEM((n * chunks, STATE, width), BF16) for n in (1, 2))
    total = pltpu.VMEM((chunks, STATE, width), F32)
    half_d, quarter_d = pltpu.VMEM((8, 2 * quarter), F32), pltpu.VMEM((8, quarter), F32)
    sem_one, sem_two = (pltpu.SemaphoreType.DMA((n * chunks, 2)) for n in (1, 2))
    incoming = pl.pallas_call(
        functools.partial(chain_kernel, chunks),
        in_specs=[pl.BlockSpec(memory_space=pltpu.VMEM)] * 2,
        out_specs=pl.BlockSpec(memory_space=pltpu.VMEM),
        out_shape=jax.ShapeDtypeStruct((STATE, channels), BF16),
        scratch_shapes=[
            twos, twos, ones, ones, total, total, ones, ones, ones, ones, twos, twos,
            half_d, half_d, quarter_d, quarter_d,
            sem_two, sem_one, sem_one, sem_one, sem_two, pltpu.SemaphoreType.DMA((2, 2)),
        ],
        compiler_params=pltpu.CompilerParams(
            collective_id=0, has_side_effects=True, vmem_limit_bytes=VMEM_LIMIT
        ),
        name="state_chain",
    )(summary, decays)

    big = pltpu.VMEM((BLOCK, channels), F32)
    return pl.pallas_call(
        functools.partial(output_kernel, groups),
        grid=(blocks,),
        in_specs=[
            lengths, tall(channels), tall(pairs), tall(channels), whole(STATE, channels), *scalars,
            whole(1, heads), whole(1, channels),
        ],
        out_specs=tall(channels),
        out_shape=jax.ShapeDtypeStruct((rows, channels), BF16),
        scratch_shapes=[
            pltpu.VMEM((STATE, channels), F32), big, pltpu.VMEM((BLOCK, channels), BF16), big, big,
            pltpu.VMEM((8, channels), F32), pltpu.VMEM((2 * repeat, wide), BF16),
        ],
        compiler_params=params,
        name="block_outputs",
    )(
        seg_lengths, xc, bcc, z_gate, incoming, dtp, dt_bias[None], decay_log[None],
        skip_gain[None], norm_gain[None],
    )


def solution(mesh):
    return jax.shard_map(
        shards,
        mesh=mesh,
        in_specs=(
            P(("groups", "seq"), "head"),
            P(("groups", "seq"), "head"),
            P(("groups", "seq"), "head", None),
            P(("groups", "seq"), "head"),
            P("head"),
            P("head"),
            P("head"),
            P(None, "head"),
            P("head"),
            P(None, "head", None),
            P("head", None),
            P("head"),
            P("groups"),
        ),
        out_specs=P(("groups", "seq"), "head"),
        check_vma=False,
    )
```

```python
import functools

import jax
import jax.numpy as jnp
from jax import lax
from jax.experimental import pallas as pl
from jax.experimental.pallas import tpu as pltpu
from jax.sharding import PartitionSpec as P

HEAD_DIM = 64
STATE = 128
BLOCK = 128
LANES = 128
TAIL = 16
CONV_LANES = 256
VMEM_LIMIT = 60 << 20
LOG2E = 1.4426950408889634
MESH = pl.DeviceIdType.MESH
F32 = jnp.float32
BF16 = jnp.bfloat16


def silu_of_half(half):
    return half + half * jnp.tanh(half)


def mm(a, b, dims):
    return lax.dot_general(a, b, (dims, ((), ())), preferred_element_type=F32)


def ids_of(starts, positions):
    found = jnp.full(positions.shape, -1, jnp.int32)
    for start in starts:
        found = jnp.where(positions >= start, start, found)
    return found


def id_of(starts, position):
    found = jnp.int32(-1)
    for start in starts:
        found = jnp.where(position >= start, start, found)
    return found


class Spot:
    def __init__(self, seg_ref, block):
        rows = pl.num_programs(0) * BLOCK
        at = lax.axis_index("seq") * rows + block * BLOCK
        starts = [jnp.int32(0)]
        for j in range(seg_ref.shape[0] - 1):
            starts.append(starts[-1] + seg_ref[j])
        self.tall = at + lax.broadcasted_iota(jnp.int32, (BLOCK, LANES), 0)
        self.tall_id = ids_of(starts, self.tall)
        row = at + lax.broadcasted_iota(jnp.int32, (1, LANES), 1)
        self.row_id = ids_of(starts, row)
        before = id_of(starts, at - 1)
        end = id_of(starts, at + BLOCK - 1)
        self.same_end = (self.row_id == end).astype(F32)
        self.alive = (self.row_id == before).astype(F32)
        self.alive_end = (end == before).astype(F32)


def column(row):
    n = row.shape[1]
    i = lax.broadcasted_iota(jnp.int32, (n, n), 0)
    j = lax.broadcasted_iota(jnp.int32, (n, n), 1)
    return jnp.sum(jnp.where(i == j, row, 0.0), axis=1, keepdims=True)


def steps_of(dtp_ref, dtb_ref, dec_ref):
    raw = dtp_ref[...].astype(F32) + column(dtb_ref[...])
    dt = jnp.maximum(raw, 0.0) + jnp.log1p(jnp.exp(-jnp.abs(raw)))
    la = (-LOG2E * column(jnp.exp(dec_ref[...]))) * dt
    s = lax.broadcasted_iota(jnp.int32, (BLOCK, BLOCK), 0)
    t = lax.broadcasted_iota(jnp.int32, (BLOCK, BLOCK), 1)
    upper = (s <= t).astype(F32).astype(BF16)
    n = la.shape[0]
    parts, rest = [], la
    for _ in range(3):
        parts.append(rest.astype(BF16))
        rest = rest - parts[-1].astype(F32)
    sums = mm(jnp.concatenate(parts, axis=0), upper, ((1,), (0,)))
    return dt, sums[0:n] + (sums[n : 2 * n] + sums[2 * n : 3 * n])


def fill_spread(e_ref):
    twice, wide = e_ref.shape
    row = lax.broadcasted_iota(jnp.int32, (twice, wide), 0)
    lane = lax.broadcasted_iota(jnp.int32, (twice, wide), 1)
    e_ref[...] = (lane // HEAD_DIM == row % (twice // 2)).astype(F32).astype(BF16)


def expand(value, e_ref):
    hi = value.astype(BF16)
    lo = (value - hi.astype(F32)).astype(BF16)
    return mm(jnp.concatenate([hi, lo], axis=0), e_ref[...], ((0,), (0,)))


def shift_matrix(within):
    t = lax.broadcasted_iota(jnp.int32, (BLOCK, TAIL + BLOCK), 0)
    i = lax.broadcasted_iota(jnp.int32, (BLOCK, TAIL + BLOCK), 1)
    steps = [((i == t + (TAIL - 3 + k)) & (within[:, 0:1] >= 3 - k)).astype(F32) for k in range(3)]
    return jnp.concatenate(steps, axis=0).astype(BF16)


def conv_tile(dst, halo, shift, cols, out, weights, bias):
    src = halo[:, cols]
    past = mm(shift, src, ((1,), (0,)))
    own = src[TAIL:, :].astype(F32)
    half = 0.5 * bias + (0.5 * weights[3]) * own
    for k in range(3):
        half = half + (0.5 * weights[k]) * past[k * BLOCK : (k + 1) * BLOCK]
    value = silu_of_half(half).astype(BF16)
    dst[:, out] = value
    return value


def tiles(start, width):
    return [slice(start + j, start + j + LANES) for j in range(0, width, LANES)]


def local_kernel(
    groups, seg_ref, x_ref, bc_ref, tail_ref, dtp_ref, dtb_ref, dec_ref,
    wx_ref, bx_ref, wbc_ref, bbc_ref,
    xc_ref, bcc_ref, s_ref, d_ref, dt_ref, cum_ref, upd_ref, xhalo, bhalo, scaled, e_ref,
):
    b = pl.program_id(0)
    channels = x_ref.shape[1]
    wide = channels // groups
    repeat = dtp_ref.shape[0] // groups

    @pl.when(b == 0)
    def _():
        fill_spread(e_ref)
        s_ref[...] = jnp.zeros(s_ref.shape, F32)
        d_ref[...] = jnp.ones(d_ref.shape, F32)
        xhalo[0:TAIL, :] = tail_ref[:, 0:channels]
        bhalo[0:TAIL, :] = tail_ref[:, channels:]

    @pl.when(b > 0)
    def _():
        xhalo[0:TAIL, :] = xhalo[BLOCK : BLOCK + TAIL, :]
        bhalo[0:TAIL, :] = bhalo[BLOCK : BLOCK + TAIL, :]

    xhalo[TAIL:, :] = x_ref[...]
    bhalo[TAIL:, :] = bc_ref[...]
    spot = Spot(seg_ref, b)
    shift = shift_matrix(spot.tall - spot.tall_id)
    dt, cum = steps_of(dtp_ref, dtb_ref, dec_ref)
    dt_ref[...] = dt
    cum_ref[...] = cum
    last = cum[:, BLOCK - 1 : BLOCK]
    tail_weight = jnp.exp2(last - cum) * dt * spot.same_end
    end_decay = jnp.exp2(jnp.broadcast_to(last, cum.shape)) * spot.alive_end
    for g in range(groups):
        heads = slice(g * repeat, (g + 1) * repeat)
        lanes = slice(g * wide, (g + 1) * wide)
        sl = slice(g * 2 * STATE, (g + 1) * 2 * STATE)
        weights = [wbc_ref[k, g : g + 1, :] for k in range(4)]
        conv_tile(bcc_ref, bhalo, shift, sl, sl, weights, bbc_ref[g : g + 1, :])
        tailw = expand(tail_weight[heads], e_ref)
        decay = expand(end_decay[heads, 0:8], e_ref)
        for j in range(0, wide, CONV_LANES):
            sl = slice(g * wide + j, g * wide + j + CONV_LANES)
            weights = [wx_ref[k : k + 1, sl] for k in range(4)]
            value = conv_tile(xc_ref, xhalo, shift, sl, sl, weights, bx_ref[0:1, sl])
            scaled[:, sl] = (value.astype(F32) * tailw[:, j : j + CONV_LANES]).astype(BF16)
        b_part = bcc_ref[:, g * 2 * STATE : g * 2 * STATE + STATE]
        update = mm(b_part, scaled[:, lanes], ((0,), (0,)))
        upd_ref[:, lanes] = update
        s_ref[:, lanes] = decay[0:1] * s_ref[:, lanes] + update
        d_ref[:, lanes] = decay * d_ref[:, lanes]


def chain_kernel(
    chunks, s_ref, d_ref, in_ref, give1, take1, give2, take2, total1, total2, sent, arrive,
    back2, home2, back1, home1, hold_d1, both_d1, hold_d2, both_d2, sem1, sem2, sem3, sem4, sem5, dsem,
):
    peers = lax.axis_size("seq")
    me = lax.axis_index("seq")
    core, pair, link, links = lax.rem(me, 2), lax.rem(me // 2, 2), me // 4, peers // 4
    low1, low2 = core == 0, pair == 0
    half = s_ref.shape[1] // 2
    quarter = half // 2
    width = quarter // chunks
    near, far = me + 1 - 2 * core, me + 2 - 4 * pair
    following = lax.rem(me + 4, peers)
    barrier = pltpu.get_barrier_semaphore()
    for peer in (near, far, following, lax.rem(me + peers - 4, peers)):
        pl.semaphore_signal(barrier, inc=1, device_id={"seq": peer}, device_id_type=MESH)
    pl.semaphore_wait(barrier, 4)

    def lanes(which, k):
        return pl.ds(pl.multiple_of(which * half + k * width, LANES), width)

    def inner(k):
        return pl.ds(pl.multiple_of(k * width, LANES), width)

    def copy(src, dst, sems, peer):
        return pltpu.make_async_remote_copy(
            src_ref=src, dst_ref=dst, send_sem=sems.at[0], recv_sem=sems.at[1],
            device_id={"seq": peer}, device_id_type=MESH,
        )

    def copy1(k):
        return copy(give1.at[k], take1.at[k], sem1.at[k], near)

    def copy2(k):
        return copy(give2.at[k], take2.at[k], sem2.at[k], far)

    def copy3(k):
        return copy(sent.at[k], arrive.at[k], sem3.at[k], following)

    def copy4(k):
        return copy(back2.at[k], home2.at[k], sem4.at[k], far)

    def copy5(k):
        return copy(back1.at[k], home1.at[k], sem5.at[k], near)

    def half_lanes(which):
        return pl.ds(pl.multiple_of(which * half, LANES), half)

    def quarter_lanes(which):
        return pl.ds(pl.multiple_of(which * quarter, LANES), quarter)

    dcopy1 = copy(d_ref.at[:, half_lanes(1 - core)], hold_d1, dsem.at[0], near)
    dcopy2 = copy(both_d1.at[:, quarter_lanes(1 - pair)], hold_d2, dsem.at[1], far)
    dcopy1.start()
    theirs, ours = (1 - pair) * chunks, pair * chunks
    order = [theirs + k for k in range(chunks)] + [ours + k for k in range(chunks)]
    for k in order:
        give1[k] = s_ref[:, lanes(1 - core, k)].astype(BF16)
        copy1(k).start()
    dcopy1.wait()
    both_d1[...] = d_ref[:, half_lanes(core)] * hold_d1[...]
    dcopy2.start()

    def merge1(k):
        copy1(k).wait()
        mine, other = s_ref[:, lanes(core, k)], take1[k].astype(F32)
        d_late = jnp.where(low1, hold_d1[0:1, inner(k)], d_ref[0:1, lanes(core, k)])
        return d_late * jnp.where(low1, mine, other) + jnp.where(low1, other, mine)

    for k in range(chunks):
        give2[k] = merge1(theirs + k).astype(BF16)
        copy2(k).start()
    for k in range(chunks):
        total1[k] = merge1(ours + k)
    dcopy2.wait()
    both_d2[...] = both_d1[:, quarter_lanes(pair)] * hold_d2[...]

    def part(k):
        return slice(k * width, (k + 1) * width)

    for k in range(chunks):
        copy2(k).wait()
        mine, other = total1[k], take2[k].astype(F32)
        d_late = jnp.where(low2, hold_d2[0:1, part(k)], both_d1[0:1, inner(ours + k)])
        total2[k] = d_late * jnp.where(low2, mine, other) + jnp.where(low2, other, mine)

        @pl.when(link == 0)
        def _():
            sent[k] = total2[k].astype(BF16)
            copy3(k).start()

    def hand_over(k, into):
        mine, other = s_ref[:, lanes(core, k)], take1[k].astype(F32)
        d_early = jnp.where(low1, d_ref[0:1, lanes(core, k)], hold_d1[0:1, inner(k)])
        passed = d_early * into + jnp.where(low1, mine, other)
        in_ref[:, lanes(core, k)] = jnp.where(low1, into, passed).astype(BF16)
        back1[k] = jnp.where(low1, passed, into).astype(BF16)
        copy5(k).start()

    for k in range(chunks):

        @pl.when(link == 0)
        def _():
            arrive[k] = jnp.zeros((STATE, width), BF16)

        @pl.when(link > 0)
        def _():
            copy3(k).wait_recv()

        into = arrive[k].astype(F32)

        @pl.when((link > 0) & (link < links - 1))
        def _():
            sent[k] = (both_d2[0:1, part(k)] * into + total2[k]).astype(BF16)
            copy3(k).start()

        mine, other = total1[k], take2[k].astype(F32)
        d_early = jnp.where(low2, both_d1[0:1, inner(ours + k)], hold_d2[0:1, part(k)])
        passed = d_early * into + jnp.where(low2, mine, other)
        back2[k] = jnp.where(low2, passed, into).astype(BF16)
        copy4(k).start()
        hand_over(ours + k, jnp.where(low2, into, passed))
    for k in range(chunks):
        copy4(k).wait()
        hand_over(theirs + k, home2[k].astype(F32))
    for k in order[chunks:] + order[:chunks]:
        copy5(k).wait()
        in_ref[:, lanes(1 - core, k)] = home1[k]
    for k in range(chunks):

        @pl.when(link < links - 1)
        def _():
            copy3(k).wait_send()


def output_kernel(
    groups, seg_ref, xc_ref, bcc_ref, z_ref, in_ref, dt_ref, cum_ref, upd_ref, skip_ref, gain_ref,
    out_ref, state, cfac, carried, gated, skip_row, e_ref,
):
    b = pl.program_id(0)
    channels = xc_ref.shape[1]
    wide = channels // groups
    repeat = dt_ref.shape[0] // groups

    @pl.when(b == 0)
    def _():
        fill_spread(e_ref)
        state[...] = in_ref[...].astype(F32)
        skip = jnp.broadcast_to(column(skip_ref[...]), (groups * repeat, LANES))
        for g in range(groups):
            rows = skip[g * repeat : (g + 1) * repeat]
            skip_row[:, g * wide : (g + 1) * wide] = expand(rows, e_ref)[0:8]

    spot = Spot(seg_ref, b)
    dt, cum = dt_ref[...], cum_ref[...]
    carry_weight = jnp.exp2(cum) * spot.alive
    lower_rows = cum - jnp.log2(dt)
    columns = jnp.transpose(cum)
    t = lax.broadcasted_iota(jnp.int32, (BLOCK, BLOCK), 0)
    s = lax.broadcasted_iota(jnp.int32, (BLOCK, BLOCK), 1)
    allowed = (s <= t) & (spot.tall_id == spot.row_id)
    lane = lax.broadcasted_iota(jnp.int32, (BLOCK, LANES), 1)
    left = lane < HEAD_DIM
    for g in range(groups):
        heads = slice(g * repeat, (g + 1) * repeat)
        lanes = slice(g * wide, (g + 1) * wide)
        cfac[:, lanes] = expand(carry_weight[heads], e_ref)
        b_part = bcc_ref[:, g * 2 * STATE : g * 2 * STATE + STATE]
        c_part = bcc_ref[:, g * 2 * STATE + STATE : (g + 1) * 2 * STATE]
        carried[:, lanes] = mm(c_part, state[:, lanes].astype(BF16), ((1,), (0,)))
        scores = jnp.where(allowed, mm(c_part, b_part, ((1,), (1,))), 0.0)
        squares = jnp.zeros((BLOCK, LANES), F32)
        for j, sl in enumerate(tiles(g * wide, wide)):
            parts = []
            for h in (g * repeat + 2 * j, g * repeat + 2 * j + 1):
                spread = jnp.minimum(columns[:, h : h + 1] - lower_rows[h : h + 1, :], 80.0)
                parts.append((scores * jnp.exp2(spread)).astype(BF16))
            xc = xc_ref[:, sl]
            none = jnp.zeros_like(xc)
            pair = jnp.concatenate([jnp.where(left, xc, none), jnp.where(left, none, xc)], axis=0)
            y = mm(jnp.concatenate(parts, axis=1), pair, ((1,), (0,)))
            xf = xc.astype(F32)
            full = y + cfac[:, sl] * carried[:, sl] + skip_row[0:1, sl] * xf
            held = full * silu_of_half(0.5 * z_ref[:, sl].astype(F32))
            gated[:, sl] = held
            squares = squares + held * held
        mean = jnp.sum(squares, axis=1, keepdims=True) * (1.0 / wide)
        scale = jnp.broadcast_to(lax.rsqrt(mean + 1e-05), (BLOCK, LANES))
        for sl in tiles(g * wide, wide):
            out_ref[:, sl] = (gated[:, sl] * scale * gain_ref[0:1, sl]).astype(BF16)
        state[:, lanes] = cfac[BLOCK - 1 : BLOCK, lanes] * state[:, lanes] + upd_ref[:, lanes]


def shards(
    x_proj, z_gate, bc_proj, dt_proj, dt_bias, decay_log, skip_gain,
    conv_x, bias_x, conv_bc, bias_bc, norm_gain, seg_lengths,
):
    rows, channels = x_proj.shape
    lookback = conv_x.shape[0] - 1
    heads = dt_proj.shape[1]
    groups = bc_proj.shape[1]
    repeat = heads // groups
    wide = channels // groups
    blocks = rows // BLOCK
    peers = lax.axis_size("seq")
    bc = bc_proj.reshape(rows, groups * 2 * STATE)
    tails = jnp.concatenate([x_proj[rows - TAIL :], bc[rows - TAIL :]], axis=1)
    tails = lax.ppermute(tails, "seq", [(i, i + 1) for i in range(peers - 1)])
    dtp = dt_proj.T
    tall = lambda w: pl.BlockSpec((BLOCK, w), lambda b: (b, 0))
    whole = lambda *shape: pl.BlockSpec(shape, lambda b: (0,) * len(shape))
    lengths = pl.BlockSpec(memory_space=pltpu.SMEM)
    per_head = pl.BlockSpec((heads, BLOCK), lambda b: (0, b))
    scalars = [per_head, whole(1, heads), whole(1, heads)]
    params = pltpu.CompilerParams(
        dimension_semantics=("arbitrary",), vmem_limit_bytes=VMEM_LIMIT
    )
    pairs = groups * 2 * STATE
    xc, bcc, summary, decays, dt, cum, updates = pl.pallas_call(
        functools.partial(local_kernel, groups),
        grid=(blocks,),
        in_specs=[
            lengths, tall(channels), tall(pairs), whole(TAIL, channels + pairs), *scalars,
            whole(lookback + 1, channels), whole(1, channels),
            whole(lookback + 1, groups, 2 * STATE), whole(groups, 2 * STATE),
        ],
        out_specs=[
            tall(channels), tall(pairs), whole(STATE, channels), whole(8, channels), per_head, per_head,
            tall(channels),
        ],
        out_shape=[
            jax.ShapeDtypeStruct((rows, channels), BF16),
            jax.ShapeDtypeStruct((rows, pairs), BF16),
            jax.ShapeDtypeStruct((STATE, channels), F32),
            jax.ShapeDtypeStruct((8, channels), F32),
            jax.ShapeDtypeStruct((heads, rows), F32),
            jax.ShapeDtypeStruct((heads, rows), F32),
            jax.ShapeDtypeStruct((rows, channels), F32),
        ],
        scratch_shapes=[
            pltpu.VMEM((TAIL + BLOCK, channels), BF16),
            pltpu.VMEM((TAIL + BLOCK, pairs), BF16),
            pltpu.VMEM((BLOCK, channels), BF16),
            pltpu.VMEM((2 * repeat, wide), BF16),
        ],
        compiler_params=params,
        name="local_state",
    )(
        seg_lengths, x_proj, bc, tails, dtp, dt_bias[None], decay_log[None],
        conv_x, bias_x[None], conv_bc, bias_bc,
    )

    chunks = max(1, min(8, channels // 4 // LANES))
    quarter = channels // 4
    width = quarter // chunks
    ones, twos = (pltpu.VMEM((n * chunks, STATE, width), BF16) for n in (1, 2))
    total = pltpu.VMEM((chunks, STATE, width), F32)
    half_d, quarter_d = pltpu.VMEM((8, 2 * quarter), F32), pltpu.VMEM((8, quarter), F32)
    sem_one, sem_two = (pltpu.SemaphoreType.DMA((n * chunks, 2)) for n in (1, 2))
    incoming = pl.pallas_call(
        functools.partial(chain_kernel, chunks),
        in_specs=[pl.BlockSpec(memory_space=pltpu.VMEM)] * 2,
        out_specs=pl.BlockSpec(memory_space=pltpu.VMEM),
        out_shape=jax.ShapeDtypeStruct((STATE, channels), BF16),
        scratch_shapes=[
            twos, twos, ones, ones, total, total, ones, ones, ones, ones, twos, twos,
            half_d, half_d, quarter_d, quarter_d,
            sem_two, sem_one, sem_one, sem_one, sem_two, pltpu.SemaphoreType.DMA((2, 2)),
        ],
        compiler_params=pltpu.CompilerParams(
            collective_id=0, has_side_effects=True, vmem_limit_bytes=VMEM_LIMIT
        ),
        name="state_chain",
    )(summary, decays)

    big = pltpu.VMEM((BLOCK, channels), F32)
    return pl.pallas_call(
        functools.partial(output_kernel, groups),
        grid=(blocks,),
        in_specs=[
            lengths, tall(channels), tall(pairs), tall(channels), whole(STATE, channels), per_head, per_head, tall(channels),
            whole(1, heads), whole(1, channels),
        ],
        out_specs=tall(channels),
        out_shape=jax.ShapeDtypeStruct((rows, channels), BF16),
        scratch_shapes=[
            pltpu.VMEM((STATE, channels), F32), big, big, big,
            pltpu.VMEM((8, channels), F32), pltpu.VMEM((2 * repeat, wide), BF16),
        ],
        compiler_params=params,
        name="block_outputs",
    )(
        seg_lengths, xc, bcc, z_gate, incoming, dt, cum, updates, skip_gain[None], norm_gain[None],
    )


def solution(mesh):
    return jax.shard_map(
        shards,
        mesh=mesh,
        in_specs=(
            P(("groups", "seq"), "head"),
            P(("groups", "seq"), "head"),
            P(("groups", "seq"), "head", None),
            P(("groups", "seq"), "head"),
            P("head"),
            P("head"),
            P("head"),
            P(None, "head"),
            P("head"),
            P(None, "head", None),
            P("head", None),
            P("head"),
            P("groups"),
        ),
        out_specs=P(("groups", "seq"), "head"),
        check_vma=False,
    )
```
